512 devices in a mesh: dp: 4 (over x), mp: 128 (over z, y, core).
Axes of the slice: x: 4, y: 4, z: 16, core: 2. Of those that a mesh axis runs over, the one named last changes fastest.
Arguments:
- acts: bfloat16 [8192, 16384], P('dp', 'mp'), may hold values from -6 to 6
- diag_weight: bfloat16 [7, 16384, 128], P(None, 'mp'), may hold values from -0.375 to 0.375
- cross_weight: bfloat16 [7, 16384, 128], P(None, 'mp'), may hold values from -0.375 to 0.375
- low_in: bfloat16 [16384, 64], P('mp'), may hold values from -0.046875 to 0.046875
- low_out: bfloat16 [64, 16384], P(None, 'mp'), may hold values from -0.75 to 0.75
- cotangent: bfloat16 [8192, 16384], P('dp', 'mp'), may hold values from -6 to 6
Outputs:
- output: bfloat16 [8192, 16384], P('dp', 'mp')
- grad_acts: bfloat16 [8192, 16384], P('dp', 'mp')
- grad_diag: float32 [7, 16384, 128], P(None, 'mp')
- grad_cross: float32 [7, 16384, 128], P(None, 'mp')
- grad_low_in: float32 [16384, 64], P('mp')
- grad_low_out: float32 [64, 16384], P(None, 'mp')
The draws below stay inside these ranges and needn't reach their ends.
All inputs are finite; a program needn't handle non-finite values.
Results may differ from the reference program's by a relative error of at most 0.019.
Values may be sent and summed in bfloat16 or wider, within the bound.
A program may use at most 64 MiB of HBM per device.

```python
import jax
import jax.numpy as jnp
import numpy as np

FF = 16384
RANK = 64
TOKENS = 8192
BLK = 128
SECTIONS = 7
N_MP = 128


def level_of(stream_key, shape, split, low, top_value):
    gain, own = 1.0, jax.random.fold_in(stream_key, 6)
    for axis_at, shards_of in split:
        heights = jnp.exp(jax.random.uniform(jax.random.fold_in(own, axis_at), (shards_of,), jnp.float32, low / len(split), top_value / len(split)))
        gain = gain * jnp.repeat(heights, shape[axis_at] // shards_of).reshape([-1 if axis == axis_at else 1 for axis in range(len(shape))])
    return gain


def noise(own_key, shape, scale, limit, pieces=(), dtype=jnp.bfloat16):
    level = level_of(own_key, shape, pieces, -0.22, 0.18) if pieces else 1.0
    array = jax.random.normal(own_key, shape, jnp.float32) * scale * level
    return jnp.minimum(jnp.maximum(array, -limit), limit).astype(dtype)


def setup_inputs(seed: int = 0) -> dict:
    arg_keys = jax.random.split(jax.random.key(seed), 7)
    return {
        "acts": noise(arg_keys[0], (TOKENS, FF), 1.0, 6.0, ((0, 4), (1, 128))),
        "diag_weight": noise(arg_keys[1], (SECTIONS, FF, BLK), (2 * BLK) ** -0.5, 0.375, ((1, 128),)),
        "cross_weight": noise(arg_keys[2], (SECTIONS, FF, BLK), (2 * BLK) ** -0.5, 0.375, ((1, 128),)),
        "low_in": noise(arg_keys[3], (FF, RANK), FF ** -0.5, 0.046875, ((0, 128),)),
        "low_out": noise(arg_keys[4], (RANK, FF), RANK ** -0.5, 0.75, ((1, 128),)),
        "cotangent": noise(arg_keys[5], (TOKENS, FF), 1.0, 6.0, ((0, 4), (1, 128))),
    }


def gelu_slope(pre, cot):
    return jax.vjp(lambda v: jax.nn.gelu(v, approximate=True), pre)[1](cot)[0]

def reference(acts, diag_weight, cross_weight, low_in, low_out, cotangent):
    blocks = N_MP
    sections = SECTIONS
    scale = float(TOKENS) ** (-0.5)
    diag_all = diag_weight.reshape(sections, blocks, BLK, BLK).astype(jnp.float32)
    cross_all = cross_weight.reshape(sections, blocks, BLK, BLK).astype(jnp.float32)
    state = acts.reshape(TOKENS, blocks, BLK)
    saved = []
    mixed = None
    for section in range(sections):
        perm = np.arange(blocks) ^ 1 << section
        saved.append(state)
        other = state[:, perm, :].astype(jnp.float32)
        fresh = jnp.einsum('tnb,nbc->tnc', state.astype(jnp.float32), diag_all[section])
        fresh = fresh + jnp.einsum('tnb,nbc->tnc', other, cross_all[section])
        if section < sections - 1:
            state = fresh.astype(jnp.bfloat16)
        else:
            mixed = fresh.reshape(TOKENS, FF)
    low = jnp.dot(acts, low_in, preferred_element_type=jnp.float32)
    low_b = low.astype(jnp.bfloat16)
    pre = mixed + jnp.dot(low_b, low_out, preferred_element_type=jnp.float32)
    output = jax.nn.gelu(pre, approximate=True).astype(jnp.bfloat16)
    d_pre = gelu_slope(pre, cotangent.astype(jnp.float32)).astype(jnp.bfloat16)
    d_low = jnp.dot(d_pre, low_out.T, preferred_element_type=jnp.float32).astype(jnp.bfloat16)
    low_back = jnp.dot(d_low, low_in.T, preferred_element_type=jnp.float32)
    grad_low_in = scale * jnp.dot(acts.T, d_low, preferred_element_type=jnp.float32)
    grad_low_out = scale * jnp.dot(low_b.T, d_pre, preferred_element_type=jnp.float32)
    upper = d_pre.reshape(TOKENS, blocks, BLK)
    grads_d = [None] * sections
    grads_c = [None] * sections
    grad_acts = None
    for section in range(sections - 1, -1, -1):
        perm = np.arange(blocks) ^ 1 << section
        below = saved[section].astype(jnp.float32)
        other = saved[section][:, perm, :].astype(jnp.float32)
        upper_f = upper.astype(jnp.float32)
        grads_d[section] = scale * jnp.einsum('tnb,tnc->nbc', below, upper_f)
        grads_c[section] = scale * jnp.einsum('tnb,tnc->nbc', other, upper_f)
        sent = jnp.einsum('tnc,nbc->tnb', upper_f, cross_all[section]).astype(jnp.bfloat16)
        back = jnp.einsum('tnc,nbc->tnb', upper_f, diag_all[section]) + sent[:, perm, :].astype(jnp.float32)
        if section > 0:
            upper = back.astype(jnp.bfloat16)
        else:
            grad_acts = (back.reshape(TOKENS, FF) + low_back).astype(jnp.bfloat16)
    grad_diag = jnp.stack(grads_d).reshape(sections, FF, BLK)
    grad_cross = jnp.stack(grads_c).reshape(sections, FF, BLK)
    return (output, grad_acts, grad_diag, grad_cross, grad_low_in, grad_low_out)
```

```python
import jax
import jax.numpy as jnp
from jax import lax
from jax.sharding import PartitionSpec as P


def swapped(block, axis, stride):
    count = lax.axis_size(axis)
    route = []
    for low in range(count):
        high = low | 1 << stride
        if high != low and high < count:
            route += [(low, high), (high, low)]
    return lax.ppermute(block, axis, route)


def gelu_slope(pre, cot):
    return jax.vjp(lambda v: jax.nn.gelu(v, approximate=True), pre)[1](cot)[0]


def summed(partial):
    piece = lax.psum_scatter(partial, "mp", scatter_dimension=0, tiled=True)
    return lax.all_gather(piece.astype(jnp.bfloat16), "mp", axis=0, tiled=True)


def rank_total(acts, low_in):
    partial_low = jnp.dot(acts, low_in, preferred_element_type=jnp.float32)
    return summed(partial_low)


def per_device(acts, diag_weight, cross_weight, low_in, low_out, cotangent):
    sections = lax.axis_size("mp").bit_length() - 1
    scale = float(acts.shape[0] * lax.axis_size("dp")) ** (-0.5)
    low = None
    state = acts
    saved = []
    partners = []
    mixed = None
    for section in range(sections):
        other = swapped(state, "mp", section)
        saved.append(state)
        partners.append(other)
        fresh = jnp.dot(state, diag_weight[section], preferred_element_type=jnp.float32)
        fresh = fresh + jnp.dot(other, cross_weight[section], preferred_element_type=jnp.float32)
        if section < sections - 1:
            state = fresh.astype(jnp.bfloat16)
        else:
            mixed = fresh
    low = rank_total(acts, low_in)
    low_b = low.astype(jnp.bfloat16)
    pre = mixed + jnp.dot(low_b, low_out, preferred_element_type=jnp.float32)
    output = jax.nn.gelu(pre, approximate=True).astype(jnp.bfloat16)
    d_pre = gelu_slope(pre, cotangent.astype(jnp.float32)).astype(jnp.bfloat16)
    partial_back = jnp.dot(d_pre, low_out.T, preferred_element_type=jnp.float32)
    d_low = summed(partial_back)
    low_back = jnp.dot(d_low, low_in.T, preferred_element_type=jnp.float32)
    local_in = scale * jnp.dot(acts.T, d_low, preferred_element_type=jnp.float32)
    local_out = scale * jnp.dot(low_b.T, d_pre, preferred_element_type=jnp.float32)
    grad_low_in, grad_low_out = (
        lax.psum(local_in.astype(jnp.bfloat16), "dp").astype(jnp.float32),
        lax.psum(local_out.astype(jnp.bfloat16), "dp").astype(jnp.float32),
    )
    upper = d_pre
    grads_d = [None] * sections
    grads_c = [None] * sections
    grad_acts = None
    for section in range(sections - 1, -1, -1):
        term_d = scale * jnp.dot(saved[section].T, upper, preferred_element_type=jnp.float32)
        term_c = scale * jnp.dot(partners[section].T, upper, preferred_element_type=jnp.float32)
        term_d, term_c = (
            lax.psum(term_d.astype(jnp.bfloat16), "dp").astype(jnp.float32),
            lax.psum(term_c.astype(jnp.bfloat16), "dp").astype(jnp.float32),
        )
        grads_d[section] = term_d
        grads_c[section] = term_c
        sent = jnp.dot(upper, cross_weight[section].T, preferred_element_type=jnp.float32).astype(
            jnp.bfloat16
        )
        arrived = swapped(sent, "mp", section)
        back = jnp.dot(
            upper, diag_weight[section].T, preferred_element_type=jnp.float32
        ) + arrived.astype(jnp.float32)
        if section > 0:
            upper = back.astype(jnp.bfloat16)
        else:
            grad_acts = (back + low_back).astype(jnp.bfloat16)
    grad_diag = jnp.stack(grads_d)
    grad_cross = jnp.stack(grads_c)
    return (output, grad_acts, grad_diag, grad_cross, grad_low_in, grad_low_out)


def solution(mesh):
    placed = (
        P("dp", "mp"),
        P(None, "mp", None),
        P(None, "mp", None),
        P("mp", None),
        P(None, "mp"),
        P("dp", "mp"),
    )
    return jax.shard_map(
        per_device,
        mesh=mesh,
        in_specs=placed,
        out_specs=(
            P("dp", "mp"),
            P("dp", "mp"),
            P(None, "mp", None),
            P(None, "mp", None),
            P("mp", None),
            P(None, "mp"),
        ),
        check_vma=False,
    )
```

```python
import functools

import jax
import jax.numpy as jnp
from jax import lax
from jax.experimental import pallas as pl
from jax.experimental.pallas import tpu as pltpu
from jax.sharding import PartitionSpec as P

MESH = pl.DeviceIdType.MESH
BF = jnp.bfloat16
F32 = jnp.float32
BLK = 128
RANK = 64
ROWS = 8
NEAR = 3
FAR = 4
PIECE = 2 * BLK + RANK // FAR


def flipped(index, stride):
    return index + stride - 2 * stride * ((index // stride) % 2)


def mm(a, b):
    return lax.dot_general(a, b, (((1,), (0,)), ((), ())), preferred_element_type=F32)


def mm_nt(a, b):
    return lax.dot_general(a, b, (((1,), (1,)), ((), ())), preferred_element_type=F32)


def mm_tn(a, b):
    return lax.dot_general(a, b, (((0,), (0,)), ((), ())), preferred_element_type=F32)


def kernel(
    nx, nz, scale,
    acts, cot, diag, cross, packed_w, lin2,
    out, gacts, gdiag, gcross, glin, glout,
    near_in, near_z, far, cot_far, out_snd, out_rcv, d_snd, d_rcv,
    weights, upper, grad_snd, grad_rcv, red, rs_snd, rs_rcv, fin_snd, fin_rcv,
    near_dz, q_snd, q_rcv, sg_snd, sg_rcv, gl_snd, gl_rcv,
    lp_snd, lp_rcv, lb_snd, lb_rcv, low_u, dacc, db_snd, db_rcv, dl_snd, dl_all,
    f_send, f_recv, b_send, b_recv, w_send, w_recv, x_send, x_recv,
    a_send, a_recv, low_send, low_recv, g_send, g_recv, rs_send, rs_recv, s_send, s_recv,
):
    x = lax.axis_index("dp")
    n = lax.axis_index("mp")
    z, r = n // ROWS, n % ROWS

    def at_z(zz):
        return (x, zz * ROWS + r)

    def at_r(rr):
        return (x, z * ROWS + rr)

    def at_x(xx):
        return (xx, n)

    def send(src, dst, ssem, rsem, where):
        pltpu.make_async_remote_copy(
            src_ref=src, dst_ref=dst, send_sem=ssem, recv_sem=rsem,
            device_id=where, device_id_type=MESH,
        ).start()

    def take(ref, sem):
        pltpu.make_async_copy(ref, ref, sem).wait()

    barrier = pltpu.get_barrier_semaphore()

    def greet(count, where):
        def one(k, _):
            pl.semaphore_signal(barrier, inc=1, device_id=where(k), device_id_type=MESH)
            return 0
        lax.fori_loop(1, count, one, 0)

    greet(nz, lambda k: at_z((z + k) % nz))
    greet(ROWS, lambda k: at_r((r + k) % ROWS))
    greet(nx, lambda k: at_x((x + k) % nx))
    pl.semaphore_wait(barrier, nz + ROWS + nx - 3)

    hz = nz // 2
    half = hz * RANK

    def chunk(ref, j):
        return ref.at[j // 2, pl.ds((j % 2) * hz, hz)]

    def load(ref, j):
        return ref[j // 2, pl.ds((j % 2) * hz, hz)].reshape(half, BLK)

    def near_send(src, dst, j, section, ssem, rsem):
        send(chunk(src, j), chunk(dst, j), ssem, rsem, (x, flipped(n, 1 << section)))

    for j in range(4):
        near_send(acts, near_in.at[0], j, 0, f_send.at[0], f_recv.at[0, j])

    steps_up = nz // 2
    steps_down = nz - 1 - steps_up

    def w_pass(k):
        up, down = (z + nz - k) % nz, (z + k) % nz

        def hop(piece, where, direction):
            src = packed_w.at[x] if k == 0 else weights.at[x, piece]
            send(src, weights.at[x, piece], w_send.at[direction], w_recv.at[piece], at_z(where))

        if k < steps_up:
            hop(up, (z + 1) % nz, 0)
        if k < steps_down:
            hop(down, (z + nz - 1) % nz, 1)

    def w_take(k):
        def one(piece):
            take(weights.at[x, piece], w_recv.at[piece])
            def other(d, _):
                send(weights.at[x, piece], weights.at[x, piece], x_send.at[0], x_recv.at[x, piece], at_x((x + d) % nx))
                return 0
            lax.fori_loop(1, nx, other, 0)
        if k <= steps_up:
            one((z + nz - k) % nz)
        if k <= steps_down:
            one((z + k) % nz)

    w_pass(0)
    for q in range(FAR):
        weights[q, z] = packed_w[q]

    for j in range(2):
        zs = pl.ds(j * hz, hz)
        part = mm(acts[0, zs].reshape(half, BLK), lin2[0]) + mm(acts[1, zs].reshape(half, BLK), lin2[1])
        lp_snd[zs] = part.reshape(hz, RANK, BLK).astype(BF)

    def far_all(count, fn):
        def one(k, _):
            fn((z + k) % count)
            return 0
        lax.fori_loop(1, count, one, 0)

    far_all(nz, lambda zz: send(lp_snd.at[zz], lp_rcv.at[z], low_send.at[0], low_recv.at[0], at_z(zz)))
    lp_rcv[z] = lp_snd[z]

    def near_forward(section, src, dst, after):
        both = jnp.concatenate([diag[section], cross[section]], axis=0)
        for j in range(4):
            take(chunk(near_in.at[section], j), f_recv.at[section, j])
            fresh = mm(jnp.concatenate([load(src, j), load(near_in.at[section], j)], axis=1), both)
            dst[j // 2, pl.ds((j % 2) * hz, hz)] = fresh.astype(BF).reshape(hz, RANK, BLK)
            after(j)

    def after0(j):
        near_send(near_z.at[0], near_in.at[1], j, 1, f_send.at[1], f_recv.at[1, j])

    near_forward(0, acts, near_z.at[0], after0)

    far_all(nz, lambda zz: send(cot.at[:, zz], cot_far.at[z], a_send.at[0], a_recv.at[0], at_z(zz)))
    cot_far[z] = cot[:, z]

    def ring(k):
        if k <= steps_up:
            w_take(k)
            w_pass(k)

    def after1(j):
        near_send(near_z.at[1], near_in.at[2], j, 2, f_send.at[2], f_recv.at[2, j])
        ring(1 + j)

    near_forward(1, near_z.at[0], near_z.at[1], after1)

    take(lp_rcv.at[pl.ds(0, nz - 1)], low_recv.at[0])
    total = lp_rcv[0].astype(F32)
    for zz in range(1, nz):
        total = total + lp_rcv[zz].astype(F32)
    lb_snd[...] = total

    def plane_all(src, dst, sem):
        def one(k, _):
            send(src, dst.at[r], low_send.at[sem], low_recv.at[sem], at_r((r + k) % ROWS))
            return 0
        lax.fori_loop(1, ROWS, one, 0)

    plane_all(lb_snd, lb_rcv, 1)
    lb_rcv[r] = lb_snd[...]

    def after2(j):
        if j % 2:
            c = j // 2
            far_all(nz, lambda zz: send(near_z.at[2, c, zz], far.at[0, z, c], a_send.at[1], a_recv.at[1], at_z(zz)))
            far[0, z, c] = near_z[2, c, z]
        ring(5 + j)

    near_forward(2, near_z.at[1], near_z.at[2], after2)
    for k in range(9, steps_up + 1):
        ring(k)

    take(lb_rcv.at[pl.ds(0, ROWS - 1)], low_recv.at[1])
    total = lb_rcv[0]
    for rr in range(1, ROWS):
        total = total + lb_rcv[rr]
    low_u[0:RANK] = total[:, :RANK].astype(BF)
    low_u[RANK:BLK] = total[:, RANK:].astype(BF)

    take(far.at[0, pl.ds(0, nz - 1)], a_recv.at[1])

    def weights_ready(q):
        @pl.when(x != q)
        def _():
            def one(k, _):
                piece = (z + k) % nz
                take(weights.at[q, piece], x_recv.at[q, piece])
                return 0
            lax.fori_loop(1, nz, one, 0)

    def tile(ref, b):
        return ref[b].reshape(BLK, BLK)

    def pair(ref, b, stride):
        return jnp.concatenate([tile(ref, b), tile(ref, flipped(b, stride))], axis=1)

    for q in range(FAR - 1):
        weights_ready(q)

        def forward(b, _, q=q):
            fresh = mm(pair(far.at[q], b, 1 << q), weights[q, b, 0:2 * BLK])
            far[q + 1, b] = fresh.astype(BF).reshape(2, RANK, BLK)
            return 0
        lax.fori_loop(0, nz, forward, 0, unroll=2)

    weights_ready(FAR - 1)
    take(cot_far.at[pl.ds(0, nz - 1)], a_recv.at[0])
    dacc[...] = jnp.zeros_like(dacc)
    root = 0.7978845608028654

    def last(k, _):
        b = (z + k) % nz
        lout = jnp.concatenate([weights[q, b, 2 * BLK:PIECE] for q in range(FAR)], axis=0)
        pre = mm(pair(far.at[FAR - 1], b, 1 << (FAR - 1)), weights[FAR - 1, b, 0:2 * BLK])
        pre = pre + mm(low_u[...], lout)
        square = pre * pre
        th = jnp.tanh(root * (pre * (1.0 + 0.044715 * square)))
        side = 0.5 * (1.0 + th)
        out_snd[b] = (pre * side).astype(BF).reshape(2, RANK, BLK)
        slope = side + 0.5 * pre * (1.0 - th * th) * (root * (1.0 + 3 * 0.044715 * square))
        dpre = (cot_far[b].reshape(BLK, BLK).astype(F32) * slope).astype(BF)
        upper[FAR, b] = dpre.reshape(2, RANK, BLK)
        dacc[...] += mm_nt(dpre, lout)

        @pl.when(b != z)
        def _():
            send(out_snd.at[b], out_rcv.at[:, z], a_send.at[2], a_recv.at[2], at_z(b))
        return 0

    lax.fori_loop(1, nz + 1, last, 0)
    out_rcv[:, z] = out_snd[z]
    db_snd[...] = jnp.concatenate([dacc[0:RANK], dacc[RANK:BLK]], axis=1)
    plane_all(db_snd, db_rcv, 2)
    db_rcv[r] = db_snd[...]

    for q in range(FAR - 1, -1, -1):
        def backward(k, _, q=q):
            b = (z + k) % nz
            o = flipped(b, 1 << q)
            here = tile(upper.at[q + 1], b)
            grad_snd[q, b, 0:2 * BLK] = mm_tn(pair(far.at[q], b, 1 << q), here).astype(BF)
            if q == FAR - 1:
                gl = mm_tn(low_u[...], here).astype(BF)
                for p in range(FAR):
                    grad_snd[p, b, 2 * BLK:PIECE] = gl[p * (RANK // FAR):(p + 1) * (RANK // FAR)]
            both = jnp.concatenate([weights[q, b, 0:BLK], weights[q, o, BLK:2 * BLK]], axis=1)
            back = mm_nt(jnp.concatenate([here, tile(upper.at[q + 1], o)], axis=1), both)
            upper[q, b] = back.astype(BF).reshape(2, RANK, BLK)
            if q == 0:
                @pl.when(b != z)
                def _():
                    send(upper.at[0, b], d_rcv.at[:, z], a_send.at[3], a_recv.at[3], at_z(b))
            return 0
        lax.fori_loop(1, nz + 1, backward, 0, unroll=2 if q else 1)

        @pl.when(x != q)
        def _():
            send(grad_snd.at[q], grad_rcv.at[x], g_send.at[0], g_recv.at[x], (q, n))

        if q == FAR - 1:
            take(db_rcv.at[pl.ds(0, ROWS - 1)], low_recv.at[2])
            total = db_rcv[0]
            for rr in range(1, ROWS):
                total = total + db_rcv[rr]
            dl_snd[...] = total.astype(BF)
            far_all(nz, lambda zz: send(dl_snd, dl_all.at[z], low_send.at[3], low_recv.at[3], at_z(zz)))
            dl_all[z] = dl_snd[...]
    d_rcv[:, z] = upper[0, z]

    def red_all():
        for d in range(1, nx):
            take(grad_rcv.at[(x + d) % nx], g_recv.at[(x + d) % nx])

        def one(b, _):
            total = grad_snd[x, b].astype(F32)
            for d in range(1, nx):
                total = total + grad_rcv[(x + d) % nx, b].astype(F32)
            red[b] = total.astype(BF)
            return 0
        lax.fori_loop(0, nz, one, 0)

    def rs_step(k):
        up, down = (z + steps_up + 1 - k) % nz, (z + nz - (steps_down + 1 - k)) % nz
        for direction, target, where, count in ((0, up, (z + 1) % nz, steps_up), (1, down, (z + nz - 1) % nz, steps_down)):
            if k > count:
                continue
            if k == 1:
                src = red.at[target]
            else:
                take(rs_rcv.at[direction, k - 2], rs_recv.at[direction, k - 2])
                rs_snd[direction, k - 1] = (rs_rcv[direction, k - 2].astype(F32) + red[target].astype(F32)).astype(BF)
                src = rs_snd.at[direction, k - 1]
            send(src, rs_rcv.at[direction, k - 1], rs_send.at[direction], rs_recv.at[direction, k - 1], at_z(where))

    take(d_rcv.at[:, pl.ds(0, nz - 1)], a_recv.at[3])

    def near_q(section, src, j):
        q_snd[section, j // 2, pl.ds((j % 2) * hz, hz)] = mm_nt(load(src, j), cross[section]).astype(BF).reshape(hz, RANK, BLK)
        near_send(q_snd.at[section], q_rcv.at[section], j, section, b_send.at[section], b_recv.at[section, j])

    def near_grad(section, state, dz):
        total = None
        for j in range(4):
            lhs = jnp.concatenate([load(state, j), load(near_in.at[section], j)], axis=1)
            part = mm_tn(lhs, load(dz, j))
            total = part if total is None else total + part
        sg_snd[section] = total.astype(BF)
        def other(d, _):
            send(sg_snd.at[section], sg_rcv.at[x, section], s_send.at[0], s_recv.at[section, x], at_x((x + d) % nx))
            return 0
        lax.fori_loop(1, nx, other, 0)
        sg_rcv[x, section] = sg_snd[section]

    for j in range(4):
        near_q(2, d_rcv, j)
    near_grad(2, near_z.at[1], d_rcv)
    red_all()
    rs_step(1)

    def near_back(section, src, j):
        take(chunk(q_rcv.at[section], j), b_recv.at[section, j])
        return mm_nt(load(src, j), diag[section]) + load(q_rcv.at[section], j).astype(F32)

    for section, src, state in ((2, d_rcv, None), (1, near_dz.at[1], near_z.at[0])):
        dst = near_dz.at[section - 1]
        for j in range(4):
            back = near_back(section, src, j)
            dst[j // 2, pl.ds((j % 2) * hz, hz)] = back.astype(BF).reshape(hz, RANK, BLK)
            near_q(section - 1, dst, j)
        if section == 2:
            near_grad(1, near_z.at[0], near_dz.at[1])
        else:
            near_grad(0, acts, near_dz.at[0])
        for k in range(2 + 3 * (2 - section), 5 + 3 * (2 - section)):
            if k <= steps_up:
                rs_step(k)

    take(dl_all.at[pl.ds(0, nz - 1)], low_recv.at[3])
    total = None
    for j in range(2):
        zs = pl.ds(j * hz, hz)
        dl = dl_all[zs].reshape(half, BLK)
        part = (mm_tn(dl, acts[0, zs].reshape(half, BLK))[0:RANK]
                + mm_tn(dl, acts[1, zs].reshape(half, BLK))[RANK:BLK])
        total = part if total is None else total + part
    gl_snd[...] = total.astype(BF)
    def other(d, _):
        send(gl_snd, gl_rcv.at[x], s_send.at[1], s_recv.at[NEAR, x], at_x((x + d) % nx))
        return 0
    lax.fori_loop(1, nx, other, 0)
    gl_rcv[x] = gl_snd[...]

    for k in range(8, steps_up + 1):
        rs_step(k)

    for j in range(4):
        zs = pl.ds((j % 2) * hz, hz)
        back = near_back(0, near_dz.at[0], j) + mm_nt(dl_all[zs].reshape(half, BLK), lin2[j // 2])
        gacts[j // 2, zs] = back.astype(BF).reshape(hz, RANK, BLK)

    take(rs_rcv.at[0, steps_up - 1], rs_recv.at[0, steps_up - 1])
    total = red[z].astype(F32) + rs_rcv[0, steps_up - 1].astype(F32)
    if steps_down:
        take(rs_rcv.at[1, steps_down - 1], rs_recv.at[1, steps_down - 1])
        total = total + rs_rcv[1, steps_down - 1].astype(F32)
    fin_snd[...] = total.astype(BF)
    def final(d, _):
        send(fin_snd, fin_rcv.at[x], g_send.at[1], g_recv.at[nx + x], at_x((x + d) % nx))
        return 0
    lax.fori_loop(1, nx, final, 0)
    fin_rcv[x] = fin_snd[...]

    take(out_rcv.at[:, pl.ds(0, nz - 1)], a_recv.at[2])
    out[...] = out_rcv[...]

    for section in range(NEAR):
        for d in range(1, nx):
            take(sg_rcv.at[(x + d) % nx, section], s_recv.at[section, (x + d) % nx])
        total = sg_rcv[0, section].astype(F32)
        for xx in range(1, nx):
            total = total + sg_rcv[xx, section].astype(F32)
        total = total * scale
        gdiag[section] = total[0:BLK]
        gcross[section] = total[BLK:2 * BLK]
    for d in range(1, nx):
        take(gl_rcv.at[(x + d) % nx], s_recv.at[NEAR, (x + d) % nx])
    total = gl_rcv[0].astype(F32)
    for xx in range(1, nx):
        total = total + gl_rcv[xx].astype(F32)
    glin[...] = total * scale
    for d in range(1, nx):
        take(fin_rcv.at[(x + d) % nx], g_recv.at[nx + (x + d) % nx])
    for q in range(FAR):
        total = fin_rcv[q].astype(F32) * scale
        gdiag[NEAR + q] = total[0:BLK]
        gcross[NEAR + q] = total[BLK:2 * BLK]
        glout[q] = total[2 * BLK:PIECE]

    for section in range(NEAR):
        take(near_in.at[section], f_send.at[section])
        take(q_snd.at[section], b_send.at[section])
    take(weights.at[0, pl.ds(0, steps_up)], w_send.at[0])
    if steps_down:
        take(weights.at[0, pl.ds(0, steps_down)], w_send.at[1])
        take(rs_snd.at[1, pl.ds(0, steps_down)], rs_send.at[1])
    take(rs_snd.at[0, pl.ds(0, steps_up)], rs_send.at[0])
    take(weights.at[pl.ds(0, nx - 1), pl.ds(0, nz - 1)], x_send.at[0])
    take(cot_far.at[pl.ds(0, nz - 1)], a_send.at[0])
    take(far.at[0, pl.ds(0, nz - 1)], a_send.at[1])
    take(out_snd.at[pl.ds(0, nz - 1)], a_send.at[2])
    take(upper.at[0, pl.ds(0, nz - 1)], a_send.at[3])
    take(lp_snd.at[pl.ds(0, nz - 1)], low_send.at[0])
    take(lb_rcv.at[pl.ds(0, ROWS - 1)], low_send.at[1])
    take(db_rcv.at[pl.ds(0, ROWS - 1)], low_send.at[2])
    take(dl_all.at[pl.ds(0, nz - 1)], low_send.at[3])
    take(grad_snd.at[pl.ds(0, FAR - 1)], g_send.at[0])
    take(fin_rcv.at[pl.ds(0, nx - 1)], g_send.at[1])
    take(sg_rcv.at[pl.ds(0, nx - 1)], s_send.at[0])
    take(gl_rcv.at[pl.ds(0, nx - 1)], s_send.at[1])


def per_device(nx, nz, acts, diag, cross, low_in, low_out, cot):
    tokens = acts.shape[0]
    scale = float(tokens * nx) ** (-0.5)
    rank = low_in.shape[1]
    split = (2, nz, RANK, BLK)
    packed_w = jnp.concatenate(
        [diag[NEAR:], cross[NEAR:], low_out.reshape(FAR, rank // FAR, BLK)], axis=1
    )
    zero = jnp.zeros_like(low_in)
    lin2 = jnp.stack([jnp.concatenate([low_in, zero], 1), jnp.concatenate([zero, low_in], 1)])
    vm = pltpu.VMEM
    dma = pltpu.SemaphoreType.DMA
    far = (nz, 2, RANK, BLK)
    low = (RANK, BLK)
    scratch = [
        vm((NEAR, *split), BF), vm((NEAR, *split), BF), vm((FAR, *far), BF), vm(far, BF), vm(far, BF), vm(split, BF), vm((8, 128), BF), vm(split, BF),
        vm((FAR, nz, PIECE, BLK), BF), vm((FAR + 1, *far), BF), vm((FAR, nz, PIECE, BLK), BF), vm((nx, nz, PIECE, BLK), BF), vm((nz, PIECE, BLK), BF),
        vm((2, nz // 2, PIECE, BLK), BF), vm((2, nz // 2, PIECE, BLK), BF), vm((PIECE, BLK), BF), vm((nx, PIECE, BLK), BF),
        vm((2, *split), BF), vm((NEAR, *split), BF), vm((NEAR, *split), BF), vm((NEAR, 2 * BLK, BLK), BF), vm((nx, NEAR, 2 * BLK, BLK), BF), vm(low, BF), vm((nx, *low), BF),
        vm((nz, *low), BF), vm((nz, *low), BF), vm(low, F32), vm((ROWS, *low), F32), vm((BLK, RANK), BF), vm((BLK, RANK), F32), vm(low, F32), vm((ROWS, *low), F32), vm(low, BF), vm((nz, *low), BF),
        dma((NEAR,)), dma((NEAR, 4)), dma((NEAR,)), dma((NEAR, 4)), dma((2,)), dma((nz,)), dma((1,)), dma((FAR, nz)),
        dma((4,)), dma((4,)), dma((4,)), dma((4,)), dma((2,)), dma((2 * nx,)), dma((2,)), dma((2, nz // 2)), dma((2,)), dma((NEAR + 1, nx)),
    ]
    whole = pl.BlockSpec(memory_space=pltpu.VMEM)
    out, gacts, gdiag, gcross, glin, glout = pl.pallas_call(
        functools.partial(kernel, nx, nz, scale),
        out_shape=(
            jax.ShapeDtypeStruct(split, BF),
            jax.ShapeDtypeStruct(split, BF),
            jax.ShapeDtypeStruct(diag.shape, F32),
            jax.ShapeDtypeStruct(cross.shape, F32),
            jax.ShapeDtypeStruct(low, F32),
            jax.ShapeDtypeStruct((FAR, RANK // FAR, BLK), F32),
        ),
        in_specs=[whole] * 6,
        out_specs=(whole,) * 6,
        scratch_shapes=scratch,
        compiler_params=pltpu.CompilerParams(
            collective_id=0, has_side_effects=True, vmem_limit_bytes=60 << 20
        ),
    )(acts.reshape(split), cot.reshape(split), diag, cross, packed_w, lin2)
    return (
        out.reshape(acts.shape), gacts.reshape(acts.shape), gdiag, gcross, glin.T, glout.reshape(low_out.shape),
    )


def solution(mesh):
    nx = mesh.shape["dp"]
    nz = mesh.shape["mp"] // ROWS
    return jax.shard_map(
        functools.partial(per_device, nx, nz),
        mesh=mesh,
        in_specs=(
            P("dp", "mp"), P(None, "mp", None), P(None, "mp", None),
            P("mp", None), P(None, "mp"), P("dp", "mp"),
        ),
        out_specs=(
            P("dp", "mp"), P("dp", "mp"), P(None, "mp", None),
            P(None, "mp", None), P("mp", None), P(None, "mp"),
        ),
        check_vma=False,
    )
```

```python
import functools

import jax
import jax.numpy as jnp
from jax import lax
from jax.experimental import pallas as pl
from jax.experimental.pallas import tpu as pltpu
from jax.sharding import PartitionSpec as P

MESH = pl.DeviceIdType.MESH
BF = jnp.bfloat16
F32 = jnp.float32
BLK = 128
RANK = 64
ROWS = 8
NEAR = 3
FAR = 4
PIECE = 2 * BLK + RANK // FAR


def flipped(index, stride):
    return index + stride - 2 * stride * ((index // stride) % 2)


def mm(a, b):
    return lax.dot_general(a, b, (((1,), (0,)), ((), ())), preferred_element_type=F32)


def mm_nt(a, b):
    return lax.dot_general(a, b, (((1,), (1,)), ((), ())), preferred_element_type=F32)


def mm_tn(a, b):
    return lax.dot_general(a, b, (((0,), (0,)), ((), ())), preferred_element_type=F32)


def kernel(
    nx, nz, scale,
    acts, cot, diag, cross, packed_w, lin2,
    out, gacts, gdiag, gcross, glin, glout,
    near_in, near_z, far, cot_far, out_snd, out_rcv, d_rcv,
    weights, upper, grad_snd, grad_rcv, rs_snd, rs_rcv, fin_snd, fin_rcv,
    near_dz, q_snd, q_rcv, sg_snd, sg_rcv, gl_snd, gl_rcv,
    lp_snd, lp_rcv, lb_snd, lb_rcv, low_u, dacc, db_snd, db_rcv, dl_snd, dl_all,
    f_send, f_recv, b_send, b_recv, w_send, w_recv, x_send, x_recv,
    a_send, a_recv, low_send, low_recv, g_send, g_recv, fin_recv, rs_send, rs_recv, s_send, s_recv,
):
    x = lax.axis_index("dp")
    n = lax.axis_index("mp")
    z, r = n // ROWS, n % ROWS

    def at_z(zz):
        return (x, zz * ROWS + r)

    def at_r(rr):
        return (x, z * ROWS + rr)

    def at_x(xx):
        return (xx, n)

    def send(src, dst, ssem, rsem, where):
        pltpu.make_async_remote_copy(
            src_ref=src, dst_ref=dst, send_sem=ssem, recv_sem=rsem,
            device_id=where, device_id_type=MESH,
        ).start()

    def take(ref, sem):
        pltpu.make_async_copy(ref, ref, sem).wait()

    barrier = pltpu.get_barrier_semaphore()

    def greet(count, where):
        def one(k, _):
            pl.semaphore_signal(barrier, inc=1, device_id=where(k), device_id_type=MESH)
            return 0
        lax.fori_loop(1, count, one, 0)

    greet(nz, lambda k: at_z((z + k) % nz))
    greet(ROWS, lambda k: at_r((r + k) % ROWS))
    greet(nx, lambda k: at_x((x + k) % nx))
    pl.semaphore_wait(barrier, nz + ROWS + nx - 3)

    hz = nz // 2
    half = hz * RANK

    def chunk(ref, j):
        return ref.at[j // 2, pl.ds((j % 2) * hz, hz)]

    def load(ref, j):
        return ref[j // 2, pl.ds((j % 2) * hz, hz)].reshape(half, BLK)

    def near_send(src, dst, j, section, ssem, rsem):
        send(chunk(src, j), chunk(dst, j), ssem, rsem, (x, flipped(n, 1 << section)))

    for j in range(4):
        near_send(acts, near_in.at[0], j, 0, f_send.at[0], f_recv.at[0, j])

    steps_up = nz // 2
    steps_down = nz - 1 - steps_up

    def w_pass(k):
        up, down = (z + nz - k) % nz, (z + k) % nz

        def hop(piece, where, direction):
            src = packed_w.at[x] if k == 0 else weights.at[x, piece]
            send(src, weights.at[x, piece], w_send.at[direction], w_recv.at[piece], at_z(where))

        if k < steps_up:
            hop(up, (z + 1) % nz, 0)
        if k < steps_down:
            hop(down, (z + nz - 1) % nz, 1)

    def w_take(k):
        def one(piece):
            take(weights.at[x, piece], w_recv.at[piece])
            def other(d, _):
                send(weights.at[x, piece], weights.at[x, piece], x_send.at[0], x_recv.at[x, piece], at_x((x + d) % nx))
                return 0
            lax.fori_loop(1, nx, other, 0)
        if k <= steps_up:
            one((z + nz - k) % nz)
        if k <= steps_down:
            one((z + k) % nz)

    w_pass(0)

    def some(first, stop, fn):
        def one(k, _):
            fn((z + k) % nz)
            return 0
        if first < min(stop, nz):
            lax.fori_loop(first, min(stop, nz), one, 0)

    some(1, nz, lambda zz: send(cot.at[:, zz], cot_far.at[z], a_send.at[0], a_recv.at[0], at_z(zz)))
    for q in range(FAR):
        weights[q, z] = packed_w[q]

    for j in range(2):
        zs = pl.ds(j * hz, hz)
        part = mm(acts[0, zs].reshape(half, BLK), lin2[0]) + mm(acts[1, zs].reshape(half, BLK), lin2[1])
        lp_snd[zs] = part.reshape(hz, RANK, BLK).astype(BF)

    def far_all(count, fn):
        def one(k, _):
            fn((z + k) % count)
            return 0
        lax.fori_loop(1, count, one, 0)

    lp_rcv[z] = lp_snd[z]
    cot_far[z] = cot[:, z]

    def low_some(first, stop):
        some(first, stop, lambda zz: send(lp_snd.at[zz], lp_rcv.at[z], low_send.at[0], low_recv.at[0], at_z(zz)))

    def ring(k):
        if k <= steps_up:
            w_take(k)
            w_pass(k)

    def near_forward(section, src, dst, after):
        both = jnp.concatenate([diag[section], cross[section]], axis=0)
        for j in range(4):
            take(chunk(near_in.at[section], j), f_recv.at[section, j])
            fresh = mm(jnp.concatenate([load(src, j), load(near_in.at[section], j)], axis=1), both)
            dst[j // 2, pl.ds((j % 2) * hz, hz)] = fresh.astype(BF).reshape(hz, RANK, BLK)
            after(j)

    def after0(j):
        near_send(near_z.at[0], near_in.at[1], j, 1, f_send.at[1], f_recv.at[1, j])
        if j == 3:
            ring(1)

    near_forward(0, acts, near_z.at[0], after0)

    def after1(j):
        near_send(near_z.at[1], near_in.at[2], j, 2, f_send.at[2], f_recv.at[2, j])
        if j % 2:
            ring(2 + j // 2)

    near_forward(1, near_z.at[0], near_z.at[1], after1)

    def after2(j):
        if j % 2:
            c = j // 2
            far_all(nz, lambda zz: send(near_z.at[2, c, zz], far.at[0, z, c], a_send.at[1], a_recv.at[1], at_z(zz)))
            far[0, z, c] = near_z[2, c, z]
        if j < 3:
            ring(4 + j)
            low_some(1 + 5 * j, 6 + 5 * j)

    near_forward(2, near_z.at[1], near_z.at[2], after2)
    for k in range(7, steps_up + 1):
        ring(k)

    take(lp_rcv.at[pl.ds(0, nz - 1)], low_recv.at[0])
    total = lp_rcv[0].astype(F32)
    for zz in range(1, nz):
        total = total + lp_rcv[zz].astype(F32)
    lb_snd[...] = total

    def plane_all(src, dst, sem):
        def one(k, _):
            send(src, dst.at[r], low_send.at[sem], low_recv.at[sem], at_r((r + k) % ROWS))
            return 0
        lax.fori_loop(1, ROWS, one, 0)

    plane_all(lb_snd, lb_rcv, 1)
    lb_rcv[r] = lb_snd[...]

    take(far.at[0, pl.ds(0, nz - 1)], a_recv.at[1])

    def weights_ready(q):
        @pl.when(x != q)
        def _():
            def one(k, _):
                piece = (z + k) % nz
                take(weights.at[q, piece], x_recv.at[q, piece])
                return 0
            lax.fori_loop(1, nz, one, 0)

    def tile(ref, b):
        return ref[b].reshape(BLK, BLK)

    def pair(ref, b, stride):
        return jnp.concatenate([tile(ref, b), tile(ref, flipped(b, stride))], axis=1)

    for q in range(FAR - 1):
        weights_ready(q)

        def forward(b, _, q=q):
            fresh = mm(pair(far.at[q], b, 1 << q), weights[q, b, 0:2 * BLK])
            far[q + 1, b] = fresh.astype(BF).reshape(2, RANK, BLK)
            return 0
        lax.fori_loop(0, nz, forward, 0, unroll=2)

    take(lb_rcv.at[pl.ds(0, ROWS - 1)], low_recv.at[1])
    total = lb_rcv[0]
    for rr in range(1, ROWS):
        total = total + lb_rcv[rr]
    low_u[0:RANK] = total[:, :RANK].astype(BF)
    low_u[RANK:BLK] = total[:, RANK:].astype(BF)
    weights_ready(FAR - 1)
    take(cot_far.at[pl.ds(0, nz - 1)], a_recv.at[0])
    dacc[...] = jnp.zeros_like(dacc)
    root = 0.7978845608028654

    def last(k, _):
        b = (z + k) % nz
        lout = jnp.concatenate([weights[q, b, 2 * BLK:PIECE] for q in range(FAR)], axis=0)
        pre = mm(pair(far.at[FAR - 1], b, 1 << (FAR - 1)), weights[FAR - 1, b, 0:2 * BLK])
        pre = pre + mm(low_u[...], lout)
        square = pre * pre
        th = jnp.tanh(root * (pre * (1.0 + 0.044715 * square)))
        side = 0.5 * (1.0 + th)
        out_snd[b] = (pre * side).astype(BF).reshape(2, RANK, BLK)
        slope = side + 0.5 * pre * (1.0 - th * th) * (root * (1.0 + 3 * 0.044715 * square))
        dpre = (cot_far[b].reshape(BLK, BLK).astype(F32) * slope).astype(BF)
        upper[FAR, b] = dpre.reshape(2, RANK, BLK)
        dacc[...] += mm_nt(dpre, lout)

        @pl.when(b != z)
        def _():
            send(out_snd.at[b, 0], out_rcv.at[0, z], a_send.at[2], a_recv.at[2], at_z(b))
        return 0

    lax.fori_loop(1, nz + 1, last, 0)
    out_rcv[:, z] = out_snd[z]
    db_snd[...] = jnp.concatenate([dacc[0:RANK], dacc[RANK:BLK]], axis=1)
    plane_all(db_snd, db_rcv, 2)
    db_rcv[r] = db_snd[...]

    for q in range(FAR - 1, -1, -1):
        def backward(k, _, q=q):
            b = (z + k) % nz
            o = flipped(b, 1 << q)
            here = tile(upper.at[q + 1], b)
            grad_snd[q, b, 0:2 * BLK] = mm_tn(pair(far.at[q], b, 1 << q), here).astype(BF)
            if q == FAR - 1:
                gl = mm_tn(low_u[...], here).astype(BF)
                for p in range(FAR):
                    grad_snd[p, b, 2 * BLK:PIECE] = gl[p * (RANK // FAR):(p + 1) * (RANK // FAR)]
            both = jnp.concatenate([weights[q, b, 0:BLK], weights[q, o, BLK:2 * BLK]], axis=1)
            back = mm_nt(jnp.concatenate([here, tile(upper.at[q + 1], o)], axis=1), both)
            upper[q, b] = back.astype(BF).reshape(2, RANK, BLK)
            if q == 0:
                @pl.when(b != z)
                def _():
                    send(upper.at[0, b, 0], d_rcv.at[0, z], a_send.at[3], a_recv.at[3], at_z(b))
            return 0
        lax.fori_loop(1, nz + 1, backward, 0, unroll=2 if q else 1)

        @pl.when(x != q)
        def _():
            def piece(b):
                send(grad_snd.at[q, b], grad_rcv.at[x, b], g_send.at[0], g_recv.at[x, b], (q, n))

            def both_ways(i, _):
                piece((z + steps_up - i) % nz)

                @pl.when(i < steps_down)
                def _():
                    piece((z + nz - steps_down + i) % nz)
                return 0
            lax.fori_loop(0, steps_up, both_ways, 0)
            piece(z)

        if q == FAR - 1:
            take(db_rcv.at[pl.ds(0, ROWS - 1)], low_recv.at[2])
            total = db_rcv[0]
            for rr in range(1, ROWS):
                total = total + db_rcv[rr]
            dl_snd[...] = total.astype(BF)
            dl_all[z] = dl_snd[...]
    d_rcv[:, z] = upper[0, z]
    far_all(nz, lambda zz: send(upper.at[0, zz, 1], d_rcv.at[1, z], a_send.at[4], a_recv.at[4], at_z(zz)))

    def low_back_some(first, stop):
        some(first, stop, lambda zz: send(dl_snd, dl_all.at[z], low_send.at[3], low_recv.at[3], at_z(zz)))

    def out_some(first, stop):
        some(first, stop, lambda zz: send(out_snd.at[zz, 1], out_rcv.at[1, z], a_send.at[5], a_recv.at[5], at_z(zz)))

    def red(b):
        total = grad_snd[x, b].astype(F32)
        for d in range(1, nx):
            take(grad_rcv.at[(x + d) % nx, b], g_recv.at[(x + d) % nx, b])
            total = total + grad_rcv[(x + d) % nx, b].astype(F32)
        return total

    def rs_step(k):
        up, down = (z + steps_up + 1 - k) % nz, (z + nz - (steps_down + 1 - k)) % nz
        for direction, target, where, count in ((0, up, (z + 1) % nz, steps_up), (1, down, (z + nz - 1) % nz, steps_down)):
            if k > count:
                continue
            total = red(target)
            if k > 1:
                take(rs_rcv.at[direction, k - 2], rs_recv.at[direction, k - 2])
                total = total + rs_rcv[direction, k - 2].astype(F32)
            rs_snd[direction, k - 1] = total.astype(BF)
            send(rs_snd.at[direction, k - 1], rs_rcv.at[direction, k - 1], rs_send.at[direction], rs_recv.at[direction, k - 1], at_z(where))

    def near_q(section, src, j):
        q_snd[section, j // 2, pl.ds((j % 2) * hz, hz)] = mm_nt(load(src, j), cross[section]).astype(BF).reshape(hz, RANK, BLK)
        near_send(q_snd.at[section], q_rcv.at[section], j, section, b_send.at[section], b_recv.at[section, j])

    def near_grad(section, state, dz):
        total = None
        for j in range(4):
            lhs = jnp.concatenate([load(state, j), load(near_in.at[section], j)], axis=1)
            part = mm_tn(lhs, load(dz, j))
            total = part if total is None else total + part
        sg_snd[section] = total.astype(BF)
        def other(d, _):
            send(sg_snd.at[section], sg_rcv.at[x, section], s_send.at[0], s_recv.at[section, x], at_x((x + d) % nx))
            return 0
        lax.fori_loop(1, nx, other, 0)
        sg_rcv[x, section] = sg_snd[section]

    rs_step(1)
    low_back_some(1, 6)
    for j in range(4):
        if j % 2 == 0:
            take(d_rcv.at[j // 2, pl.ds(0, nz - 1)], a_recv.at[3 + j // 2])
        near_q(2, d_rcv, j)
    rs_step(2)
    low_back_some(6, 11)
    near_grad(2, near_z.at[1], d_rcv)

    def near_back(section, src, j):
        take(chunk(q_rcv.at[section], j), b_recv.at[section, j])
        return mm_nt(load(src, j), diag[section]) + load(q_rcv.at[section], j).astype(F32)

    for section, src in ((2, d_rcv), (1, near_dz.at[1])):
        dst = near_dz.at[section - 1]
        for j in range(4):
            back = near_back(section, src, j)
            dst[j // 2, pl.ds((j % 2) * hz, hz)] = back.astype(BF).reshape(hz, RANK, BLK)
            near_q(section - 1, dst, j)
            if section == 2 and j % 2:
                rs_step(3 + j // 2)
                if j == 1:
                    low_back_some(11, nz)
                else:
                    out_some(1, 5)
            if section == 1 and j < 3:
                rs_step(5 + j)
                out_some(5 + 4 * j, 9 + 4 * j)
        if section == 2:
            near_grad(1, near_z.at[0], near_dz.at[1])
    near_grad(0, acts, near_dz.at[0])

    take(dl_all.at[pl.ds(0, nz - 1)], low_recv.at[3])
    total = None
    for j in range(2):
        zs = pl.ds(j * hz, hz)
        dl = dl_all[zs].reshape(half, BLK)
        part = (mm_tn(dl, acts[0, zs].reshape(half, BLK))[0:RANK]
                + mm_tn(dl, acts[1, zs].reshape(half, BLK))[RANK:BLK])
        total = part if total is None else total + part
    gl_snd[...] = total.astype(BF)
    def other(d, _):
        send(gl_snd, gl_rcv.at[x], s_send.at[1], s_recv.at[NEAR, x], at_x((x + d) % nx))
        return 0
    lax.fori_loop(1, nx, other, 0)
    gl_rcv[x] = gl_snd[...]

    for k in range(8, steps_up + 1):
        rs_step(k)

    for j in range(4):
        zs = pl.ds((j % 2) * hz, hz)
        back = near_back(0, near_dz.at[0], j) + mm_nt(dl_all[zs].reshape(half, BLK), lin2[j // 2])
        gacts[j // 2, zs] = back.astype(BF).reshape(hz, RANK, BLK)

    take(rs_rcv.at[0, steps_up - 1], rs_recv.at[0, steps_up - 1])
    total = red(z) + rs_rcv[0, steps_up - 1].astype(F32)
    if steps_down:
        take(rs_rcv.at[1, steps_down - 1], rs_recv.at[1, steps_down - 1])
        total = total + rs_rcv[1, steps_down - 1].astype(F32)
    fin_snd[...] = total.astype(BF)
    def final(d, _):
        send(fin_snd, fin_rcv.at[x], g_send.at[1], fin_recv.at[x], at_x((x + d) % nx))
        return 0
    lax.fori_loop(1, nx, final, 0)
    fin_rcv[x] = fin_snd[...]

    take(out_rcv.at[0, pl.ds(0, nz - 1)], a_recv.at[2])
    take(out_rcv.at[1, pl.ds(0, nz - 1)], a_recv.at[5])
    out[...] = out_rcv[...]

    for section in range(NEAR):
        for d in range(1, nx):
            take(sg_rcv.at[(x + d) % nx, section], s_recv.at[section, (x + d) % nx])
        total = sg_rcv[0, section].astype(F32)
        for xx in range(1, nx):
            total = total + sg_rcv[xx, section].astype(F32)
        total = total * scale
        gdiag[section] = total[0:BLK]
        gcross[section] = total[BLK:2 * BLK]
    for d in range(1, nx):
        take(gl_rcv.at[(x + d) % nx], s_recv.at[NEAR, (x + d) % nx])
    total = gl_rcv[0].astype(F32)
    for xx in range(1, nx):
        total = total + gl_rcv[xx].astype(F32)
    glin[...] = total * scale
    for d in range(1, nx):
        take(fin_rcv.at[(x + d) % nx], fin_recv.at[(x + d) % nx])
    for q in range(FAR):
        total = fin_rcv[q].astype(F32) * scale
        gdiag[NEAR + q] = total[0:BLK]
        gcross[NEAR + q] = total[BLK:2 * BLK]
        glout[q] = total[2 * BLK:PIECE]

    for section in range(NEAR):
        take(near_in.at[section], f_send.at[section])
        take(q_snd.at[section], b_send.at[section])
    take(weights.at[0, pl.ds(0, steps_up)], w_send.at[0])
    if steps_down:
        take(weights.at[0, pl.ds(0, steps_down)], w_send.at[1])
        take(rs_snd.at[1, pl.ds(0, steps_down)], rs_send.at[1])
    take(rs_snd.at[0, pl.ds(0, steps_up)], rs_send.at[0])
    take(weights.at[pl.ds(0, nx - 1), pl.ds(0, nz - 1)], x_send.at[0])
    take(cot_far.at[pl.ds(0, nz - 1)], a_send.at[0])
    take(far.at[0, pl.ds(0, nz - 1)], a_send.at[1])
    for c in range(2):
        take(out_rcv.at[c, pl.ds(0, nz - 1)], a_send.at[2 + 3 * c])
        take(d_rcv.at[c, pl.ds(0, nz - 1)], a_send.at[3 + c])
    take(lp_snd.at[pl.ds(0, nz - 1)], low_send.at[0])
    take(lb_rcv.at[pl.ds(0, ROWS - 1)], low_send.at[1])
    take(db_rcv.at[pl.ds(0, ROWS - 1)], low_send.at[2])
    take(dl_all.at[pl.ds(0, nz - 1)], low_send.at[3])
    take(grad_snd.at[pl.ds(0, FAR - 1)], g_send.at[0])
    take(fin_rcv.at[pl.ds(0, nx - 1)], g_send.at[1])
    take(sg_rcv.at[pl.ds(0, nx - 1)], s_send.at[0])
    take(gl_rcv.at[pl.ds(0, nx - 1)], s_send.at[1])


def per_device(nx, nz, acts, diag, cross, low_in, low_out, cot):
    tokens = acts.shape[0]
    scale = float(tokens * nx) ** (-0.5)
    rank = low_in.shape[1]
    split = (2, nz, RANK, BLK)
    packed_w = jnp.concatenate(
        [diag[NEAR:], cross[NEAR:], low_out.reshape(FAR, rank // FAR, BLK)], axis=1
    )
    zero = jnp.zeros_like(low_in)
    lin2 = jnp.stack([jnp.concatenate([low_in, zero], 1), jnp.concatenate([zero, low_in], 1)])
    vm = pltpu.VMEM
    dma = pltpu.SemaphoreType.DMA
    far = (nz, 2, RANK, BLK)
    low = (RANK, BLK)
    scratch = [
        vm((NEAR, *split), BF), vm((NEAR, *split), BF), vm((FAR, *far), BF), vm(far, BF), vm(far, BF), vm(split, BF), vm(split, BF),
        vm((FAR, nz, PIECE, BLK), BF), vm((FAR + 1, *far), BF), vm((FAR, nz, PIECE, BLK), BF), vm((nx, nz, PIECE, BLK), BF),
        vm((2, nz // 2, PIECE, BLK), BF), vm((2, nz // 2, PIECE, BLK), BF), vm((PIECE, BLK), BF), vm((nx, PIECE, BLK), BF),
        vm((2, *split), BF), vm((NEAR, *split), BF), vm((NEAR, *split), BF), vm((NEAR, 2 * BLK, BLK), BF), vm((nx, NEAR, 2 * BLK, BLK), BF), vm(low, BF), vm((nx, *low), BF),
        vm((nz, *low), BF), vm((nz, *low), BF), vm(low, F32), vm((ROWS, *low), F32), vm((BLK, RANK), BF), vm((BLK, RANK), F32), vm(low, F32), vm((ROWS, *low), F32), vm(low, BF), vm((nz, *low), BF),
        dma((NEAR,)), dma((NEAR, 4)), dma((NEAR,)), dma((NEAR, 4)), dma((2,)), dma((nz,)), dma((1,)), dma((FAR, nz)),
        dma((6,)), dma((6,)), dma((4,)), dma((4,)), dma((2,)), dma((nx, nz)), dma((nx,)), dma((2,)), dma((2, nz // 2)), dma((2,)), dma((NEAR + 1, nx)),
    ]
    whole = pl.BlockSpec(memory_space=pltpu.VMEM)
    out, gacts, gdiag, gcross, glin, glout = pl.pallas_call(
        functools.partial(kernel, nx, nz, scale),
        out_shape=(
            jax.ShapeDtypeStruct(split, BF),
            jax.ShapeDtypeStruct(split, BF),
            jax.ShapeDtypeStruct(diag.shape, F32),
            jax.ShapeDtypeStruct(cross.shape, F32),
            jax.ShapeDtypeStruct(low, F32),
            jax.ShapeDtypeStruct((FAR, RANK // FAR, BLK), F32),
        ),
        in_specs=[whole] * 6,
        out_specs=(whole,) * 6,
        scratch_shapes=scratch,
        compiler_params=pltpu.CompilerParams(
            collective_id=0, has_side_effects=True, vmem_limit_bytes=60 << 20
        ),
    )(acts.reshape(split), cot.reshape(split), diag, cross, packed_w, lin2)
    return (
        out.reshape(acts.shape), gacts.reshape(acts.shape), gdiag, gcross, glin.T, glout.reshape(low_out.shape),
    )


def solution(mesh):
    nx = mesh.shape["dp"]
    nz = mesh.shape["mp"] // ROWS
    return jax.shard_map(
        functools.partial(per_device, nx, nz),
        mesh=mesh,
        in_specs=(
            P("dp", "mp"), P(None, "mp", None), P(None, "mp", None),
            P("mp", None), P(None, "mp"), P("dp", "mp"),
        ),
        out_specs=(
            P("dp", "mp"), P("dp", "mp"), P(None, "mp", None),
            P(None, "mp", None), P("mp", None), P(None, "mp"),
        ),
        check_vma=False,
    )
```
